32 devices in a mesh: snap: 8 (over y, x, core), weight: 4 (over z).
Axes of the slice: x: 2, y: 2, z: 4, core: 2. Of those that a mesh axis runs over, the one named last changes fastest.
Arguments:
- features: bfloat16 [128, 4, 4, 2, 1024], P(('snap', 'weight')), may hold values from -6 to 6
- conv_weight: bfloat16 [27, 1024, 2048], P(None, None, 'weight'), may hold values from -0.0625 to 0.0625
- dense_weight: bfloat16 [4, 2048, 2048], P(None, 'weight'), may hold values from -0.0625 to 0.0625
- probe: float32 [2048, 128], replicated, may hold values from -6 to 6
Outputs:
- latents: bfloat16 [128, 2048], P(('snap', 'weight'))
- basis: float32 [2048, 128], replicated
- coeffs: float32 [128, 128], P(('snap', 'weight'))
The draws below stay inside these ranges and needn't reach their ends.
All inputs are finite; a program needn't handle non-finite values.
Results may differ from the reference program's by a relative error of at most 0.012.
Values may be sent and summed in bfloat16 or wider, within the bound.
A program may use at most 128 MiB of HBM per device.

```python
import jax
import jax.numpy as jnp
from jax import lax

C_IN = 1024
C_OUT = 2048
LATENT = 2048
RANK = 128
ITERS = 4
SNAP_DEV = 4
SNAPS = 128
N_WEIGHT = 4


def shard_levels(stream_key, shape, shards, smallest, high):
    def one(position, blocks):
        steps = jax.random.uniform(jax.random.fold_in(jax.random.fold_in(stream_key, 6), position), (blocks,), jnp.float32, smallest / len(shards), high / len(shards))
        return jnp.repeat(jnp.exp(steps), shape[position] // blocks).reshape((-1,) + (1,) * (len(shape) - position - 1))

    level = one(*shards[0])
    for cut in shards[1:]:
        level = level * one(*cut)
    return level


def normal_values(stream_key, shape, deviation, most, split=(), dtype=jnp.bfloat16):
    result = deviation * jax.random.normal(stream_key, shape, jnp.float32)
    if split:
        result = result * shard_levels(stream_key, shape, split, -0.22, 0.18)
    return jnp.clip(result, -most, most).astype(dtype)


def setup_inputs(seed: int = 0) -> dict:
    key_list = jax.random.split(jax.random.key(seed), 5)
    features = normal_values(key_list[0], (SNAPS, 4, 4, 2, C_IN), 1.0, 6.0, ((0, 32),))
    conv_weight = normal_values(key_list[1], (27, C_IN, C_OUT), (8 * C_IN) ** -0.5, 0.0625, ((2, 4),))
    dense_weight = normal_values(key_list[2], (4, C_OUT, LATENT), (4 * C_OUT) ** -0.5, 0.0625, ((1, 4),))
    probe = normal_values(key_list[3], (LATENT, RANK), 1.0, 6.0, (), jnp.float32)
    return dict(features=features, conv_weight=conv_weight, dense_weight=dense_weight, probe=probe)


def convolve(block, kernel):
    count = block.shape[0]
    channels = block.shape[-1]
    padded = jnp.pad(block, ((0, 0), (1, 1), (1, 1), (1, 1), (0, 0)))
    taps = []
    for first in range(3):
        for second in range(3):
            for third in range(3):
                taps.append(padded[:, first:first + 3:2, second:second + 3:2, third:third + 1:2, :])
    patches = jnp.concatenate(taps, axis=-1).reshape(count * 4, 27 * channels)
    summed = jnp.dot(patches.astype(jnp.float32), kernel.reshape(27 * channels, kernel.shape[-1]).astype(jnp.float32), preferred_element_type=jnp.float32)
    return jnp.tanh(summed).astype(jnp.bfloat16).reshape(count, 4, kernel.shape[-1])

def reference(features, conv_weight, dense_weight, probe):
    group = SNAP_DEV * N_WEIGHT
    blocks = features.reshape(SNAPS // group, group, 4, 4, 2, C_IN)
    dense_flat = dense_weight.reshape(4 * C_OUT, LATENT)

    def encode(block):
        hidden = convolve(block, conv_weight)
        return jnp.dot(hidden.reshape(group, 4 * C_OUT).astype(jnp.float32), dense_flat.astype(jnp.float32), preferred_element_type=jnp.float32)
    latent_f = lax.map(encode, blocks).reshape(SNAPS, LATENT)
    highest = lax.Precision.HIGHEST
    basis = probe
    for step in range(ITERS):
        projected = jnp.dot(latent_f.astype(jnp.float32), basis.astype(jnp.float32), precision=highest, preferred_element_type=jnp.float32)
        span = jnp.dot(latent_f.T.astype(jnp.float32), projected.astype(jnp.float32), precision=highest, preferred_element_type=jnp.float32)
        gram_matrix = jnp.dot(span.T.astype(jnp.float32), span.astype(jnp.float32), precision=highest, preferred_element_type=jnp.float32)
        lower_factor = jnp.linalg.cholesky(gram_matrix)
        basis = lax.linalg.triangular_solve(lower_factor, span, left_side=False, lower=True, transpose_a=True)
    coeffs = jnp.dot(latent_f.astype(jnp.float32), basis.astype(jnp.float32), precision=highest, preferred_element_type=jnp.float32)
    return (latent_f.astype(jnp.bfloat16), basis, coeffs)
```

```python
import functools

import jax
import jax.numpy as jnp
from jax import lax
from jax.experimental import pallas as pl
from jax.experimental.pallas import tpu as pltpu
from jax.sharding import PartitionSpec as P

ITERS = 4
HI = lax.Precision.HIGHEST
def dott(a,b,ca,cb):
    return lax.dot_general(a,b,(((ca,),(cb,)),((),())),precision=HI,preferred_element_type=jnp.float32)

def inverse_factor(gram):
    rank = gram.shape[0]
    nb = rank//8
    full=(8,rank)
    groups = [gram[8*g:8*g+8,:] for g in range(nb)]
    lane = lax.broadcasted_iota(jnp.int32,full,1)
    sub = lax.broadcasted_iota(jnp.int32,full,0)
    out=[]
    def col(x,j): return jnp.broadcast_to(x[:,j:j+1],full)
    def row(x,i): return jnp.broadcast_to(x[i:i+1,:],full)
    for g in range(nb):
        panel = groups[g]
        base = 8*g
        inblk = (lane>=base)&(lane<base+8)
        X=[col(panel,base+j) for j in range(8)]
        d=[[row(X[j],i) if j<=i else None for j in range(8)] for i in range(8)]
        panelI = jnp.where(inblk, jnp.where(lane-base==sub,1.0,0.0), panel)
        acc=[row(panelI,i) for i in range(8)]
        nxt = g+1<nb
        if nxt:
            C=[col(groups[g+1],base+k) for k in range(8)]
            new = jnp.where(inblk,0.0,groups[g+1])
        l=[[None]*8 for _ in range(8)]
        r=[None]*8
        W=[None]*8
        for k in range(8):
            r[k]=lax.rsqrt(d[k][k])
            W[k]=acc[k]*r[k]
            if nxt:
                C[k]=C[k]*r[k]
                new = new - C[k]*W[k]
            for i in range(k+1,8):
                l[i][k]=d[i][k]*r[k]
            for i in range(k+1,8):
                for j in range(k+1,i+1):
                    d[i][j]=d[i][j]-l[i][k]*l[j][k]
                acc[i]=acc[i]-l[i][k]*W[k]
                if nxt: C[i]=C[i]-l[i][k]*C[k]
        t=W[0]
        for k in range(1,8):
            t=jnp.where(sub==k,W[k],t)
        out.append(jnp.where(lane<base+8,t,0.0))
        first = g+1
        if nxt:
            groups[g+1]=new
            first=g+2
        if first<nb:
            U=list(W)
            for k in range(7,-1,-1):
                U[k]=U[k]*r[k]
                for i in range(k):
                    U[i]=U[i]-l[k][i]*U[k]
            for h in range(first,nb):
                b=groups[h]
                n=jnp.where(inblk,0.0,b)
                for k in range(8):
                    n=n-col(b,base+k)*U[k]
                groups[h]=n
    return jnp.concatenate(out,axis=0)

ORTH = (2, 4)


def trace_of(square):
    shape = square.shape
    eye = lax.broadcasted_iota(jnp.int32, shape, 0) == lax.broadcasted_iota(jnp.int32, shape, 1)
    return eye, jnp.sum(jnp.sum(jnp.where(eye, square, 0.0), axis=1, keepdims=True), axis=0, keepdims=True)


def subspace_kernel(z_ref, probe_ref, basis_ref, coeffs_ref):
    z = z_ref[...]
    n = z.shape[0]
    r = probe_ref.shape[1]
    g = dott(z, z, 1, 1)
    p = dott(z, probe_ref[...], 1, 0)
    mean = trace_of(g)[1] * (1.0 / n)
    g = g * (1.0 / mean)
    for it in range(1, ITERS + 1):
        m = dott(g, p, 1, 0)
        if it in ORTH:
            gram = dott(p, m, 0, 0)
            if it < ITERS:
                eye, total = trace_of(gram)
                gram = gram + jnp.where(eye, total * (2e-6 / r), 0.0)
            inv = inverse_factor(gram)
            last = dott(p, inv, 1, 1)
            p = dott(m, inv, 1, 1)
        else:
            p = m
    scale = lax.rsqrt(mean)
    coeffs_ref[...] = p * (mean * scale)
    basis_ref[...] = dott(z_ref[...], last * scale, 0, 0)


def subspace(z, probe):
    n = z.shape[0]
    r = probe.shape[1]
    return pl.pallas_call(
        subspace_kernel,
        out_shape=(jax.ShapeDtypeStruct(probe.shape, jnp.float32), jax.ShapeDtypeStruct((n, r), jnp.float32)),
        in_specs=[pl.BlockSpec(memory_space=pltpu.VMEM)] * 2,
        out_specs=[pl.BlockSpec(memory_space=pltpu.VMEM)] * 2,
        compiler_params=pltpu.CompilerParams(vmem_limit_bytes=48 << 20),
    )(z, probe)


def conv_kernel(rows_ref, weight_ref, hidden_ref, voxel_ref, sum_ref):
    tap = pl.program_id(0)
    count, channels = voxel_ref.shape[3:]

    @pl.when(tap == 0)
    def _():
        shape = (32, count, 32 * count)
        wanted = 32 * lax.broadcasted_iota(jnp.int32, shape, 1)
        wanted = wanted + lax.broadcasted_iota(jnp.int32, shape, 0)
        chosen = jnp.where(lax.broadcasted_iota(jnp.int32, shape, 2) == wanted, 1.0, 0.0)
        chosen = chosen.reshape(32 * count, 32 * count).astype(jnp.bfloat16)
        moved = jnp.dot(chosen, rows_ref[...], preferred_element_type=jnp.float32)
        moved = moved.astype(jnp.bfloat16)
        blank = jnp.zeros((count, channels), jnp.bfloat16)
        for third in range(2):
            for edge in range(5):
                voxel_ref[0, edge, third] = blank
                voxel_ref[edge, 0, third] = blank
        for v in range(32):
            voxel_ref[v // 8 + 1, (v // 2) % 4 + 1, v % 2] = moved[v * count : (v + 1) * count]
        sum_ref[...] = jnp.zeros_like(sum_ref)

    first, second, third = tap // 6, lax.rem(tap // 2, 3), lax.rem(tap, 2)
    blocks = [voxel_ref[2 * i + first, 2 * j + second, third] for i in range(2) for j in range(2)]
    patch = jnp.concatenate(blocks, axis=0)
    sum_ref[...] += jnp.dot(patch, weight_ref[0], preferred_element_type=jnp.float32)

    @pl.when(tap == pl.num_programs(0) - 1)
    def _():
        hidden_ref[...] = jnp.tanh(sum_ref[...]).astype(hidden_ref.dtype)


def convolve(rows, conv_weight):
    channels, local_out = conv_weight.shape[1:]
    count = rows.shape[0] // 32
    hidden = pl.pallas_call(
        conv_kernel,
        grid=(18,),
        in_specs=[
            pl.BlockSpec(rows.shape, lambda t: (0, 0)),
            pl.BlockSpec((1, channels, local_out), lambda t: (3 * (t // 2) + 1 + t % 2, 0, 0)),
        ],
        out_specs=pl.BlockSpec((4 * count, local_out), lambda t: (0, 0)),
        out_shape=jax.ShapeDtypeStruct((4 * count, local_out), jnp.bfloat16),
        scratch_shapes=[
            pltpu.VMEM((5, 5, 2, count, channels), jnp.bfloat16),
            pltpu.VMEM((4 * count, local_out), jnp.float32),
        ],
        compiler_params=pltpu.CompilerParams(vmem_limit_bytes=40 << 20),
    )(rows, conv_weight)
    return hidden.reshape(4, count, local_out)


def exchange_kernel(
    partial_ref, own_ref, all_ref, landing_ref, sum_send, sum_recv, row_send, row_recv, far_send, far_recv
):
    snap, weight = lax.axis_index("snap"), lax.axis_index("weight")
    snaps, weights = all_ref.shape[0], all_ref.shape[1]

    def near(distance):
        return lax.rem(weight + distance, weights)

    def far(distance):
        return lax.rem(snap + distance, snaps)

    mesh_id = pl.DeviceIdType.MESH
    barrier = pltpu.get_barrier_semaphore()
    for d in range(1, weights):
        pl.semaphore_signal(barrier, inc=1, device_id=(snap, near(d)), device_id_type=mesh_id)
    for d in range(1, snaps):
        pl.semaphore_signal(barrier, inc=1, device_id=(far(d), weight), device_id_type=mesh_id)
    pl.semaphore_wait(barrier, weights + snaps - 2)

    copies = []
    for d in range(1, weights):
        copy = pltpu.make_async_remote_copy(
            src_ref=partial_ref.at[near(d)],
            dst_ref=landing_ref.at[d],
            send_sem=sum_send.at[d],
            recv_sem=sum_recv.at[d],
            device_id=(snap, near(d)),
            device_id_type=mesh_id,
        )
        copy.start()
        copies.append(copy)
    total = partial_ref[weight]
    for d in range(1, weights):
        copies[d - 1].wait_recv()
        total = total + landing_ref[d]
    own_ref[...] = total
    all_ref[snap, weight] = total
    for d in range(1, weights):
        copies[d - 1].wait_send()

    copies = []
    for d in range(1, weights):
        copy = pltpu.make_async_remote_copy(
            src_ref=all_ref.at[snap, weight],
            dst_ref=all_ref.at[snap, weight],
            send_sem=row_send.at[d],
            recv_sem=row_recv.at[d],
            device_id=(snap, near(d)),
            device_id_type=mesh_id,
        )
        copy.start()
        copies.append(copy)
    for copy in copies:
        copy.wait()

    copies = []
    for d in range(1, snaps):
        copy = pltpu.make_async_remote_copy(
            src_ref=all_ref.at[snap],
            dst_ref=all_ref.at[snap],
            send_sem=far_send.at[d],
            recv_sem=far_recv.at[d],
            device_id=(far(d), weight),
            device_id_type=mesh_id,
        )
        copy.start()
        copies.append(copy)
    for copy in copies:
        copy.wait()


def exchange(partial, snaps):
    weights, mine, latent_width = partial.shape
    vmem = pl.BlockSpec(memory_space=pltpu.VMEM)
    return pl.pallas_call(
        exchange_kernel,
        out_shape=(
            jax.ShapeDtypeStruct((mine, latent_width), jnp.float32),
            jax.ShapeDtypeStruct((snaps, weights, mine, latent_width), jnp.float32),
        ),
        in_specs=[vmem],
        out_specs=[vmem] * 2,
        scratch_shapes=[
            pltpu.VMEM((weights, mine, latent_width), jnp.float32),
            pltpu.SemaphoreType.DMA((weights,)),
            pltpu.SemaphoreType.DMA((weights,)),
            pltpu.SemaphoreType.DMA((weights,)),
            pltpu.SemaphoreType.DMA((weights,)),
            pltpu.SemaphoreType.DMA((snaps,)),
            pltpu.SemaphoreType.DMA((snaps,)),
        ],
        compiler_params=pltpu.CompilerParams(
            collective_id=0, has_side_effects=True, vmem_limit_bytes=32 << 20
        ),
    )(partial)


def body(features, conv_weight, dense_weight, probe):
    channels = features.shape[-1]
    mine = features.shape[0]
    snaps, weights = lax.axis_size("snap"), lax.axis_size("weight")
    rows = lax.all_gather(features.reshape(-1, channels), "weight", axis=0, tiled=True)
    hidden = convolve(rows, conv_weight)
    hidden_flat = jnp.transpose(hidden, (1, 0, 2)).reshape(hidden.shape[1], -1)
    dense_flat = dense_weight.reshape(-1, dense_weight.shape[-1])
    partial = jnp.dot(hidden_flat, dense_flat, preferred_element_type=jnp.float32)
    latent_f, everything = exchange(partial.reshape(weights, mine, -1), snaps)
    basis, coeffs = subspace(everything.reshape(-1, partial.shape[-1]), probe)
    place = lax.axis_index("snap") * weights + lax.axis_index("weight")
    own_coeffs = lax.dynamic_slice_in_dim(coeffs, place * mine, mine, 0)
    return (latent_f.astype(jnp.bfloat16), basis, own_coeffs)


def solution(mesh):
    placed = (
        P(("snap", "weight"), None, None, None, None),
        P(None, None, "weight"),
        P(None, "weight", None),
        P(),
    )
    return jax.shard_map(
        body,
        mesh=mesh,
        in_specs=placed,
        out_specs=(P(("snap", "weight"), None), P(), P(("snap", "weight"), None)),
        check_vma=False,
    )
```

```python
import functools

import jax
import jax.numpy as jnp
from jax import lax
from jax.experimental import pallas as pl
from jax.experimental.pallas import tpu as pltpu
from jax.sharding import PartitionSpec as P

ITERS = 4
HI = lax.Precision.HIGHEST
def dott(a,b,ca,cb):
    return lax.dot_general(a,b,(((ca,),(cb,)),((),())),precision=HI,preferred_element_type=jnp.float32)

def inverse_factor(gram):
    rank = gram.shape[0]
    nb = rank//8
    full=(8,rank)
    groups = [gram[8*g:8*g+8,:] for g in range(nb)]
    lane = lax.broadcasted_iota(jnp.int32,full,1)
    sub = lax.broadcasted_iota(jnp.int32,full,0)
    out=[]
    def col(x,j): return jnp.broadcast_to(x[:,j:j+1],full)
    def row(x,i): return jnp.broadcast_to(x[i:i+1,:],full)
    for g in range(nb):
        panel = groups[g]
        base = 8*g
        inblk = (lane>=base)&(lane<base+8)
        X=[col(panel,base+j) for j in range(8)]
        d=[[row(X[j],i) if j<=i else None for j in range(8)] for i in range(8)]
        panelI = jnp.where(inblk, jnp.where(lane-base==sub,1.0,0.0), panel)
        acc=[row(panelI,i) for i in range(8)]
        nxt = g+1<nb
        if nxt:
            C=[col(groups[g+1],base+k) for k in range(8)]
            new = jnp.where(inblk,0.0,groups[g+1])
        l=[[None]*8 for _ in range(8)]
        r=[None]*8
        W=[None]*8
        for k in range(8):
            r[k]=lax.rsqrt(d[k][k])
            W[k]=acc[k]*r[k]
            if nxt:
                C[k]=C[k]*r[k]
                new = new - C[k]*W[k]
            for i in range(k+1,8):
                l[i][k]=d[i][k]*r[k]
            for i in range(k+1,8):
                for j in range(k+1,i+1):
                    d[i][j]=d[i][j]-l[i][k]*l[j][k]
                acc[i]=acc[i]-l[i][k]*W[k]
                if nxt: C[i]=C[i]-l[i][k]*C[k]
        t=W[0]
        for k in range(1,8):
            t=jnp.where(sub==k,W[k],t)
        out.append(jnp.where(lane<base+8,t,0.0))
        first = g+1
        if nxt:
            groups[g+1]=new
            first=g+2
        if first<nb:
            U=list(W)
            for k in range(7,-1,-1):
                U[k]=U[k]*r[k]
                for i in range(k):
                    U[i]=U[i]-l[k][i]*U[k]
            for h in range(first,nb):
                b=groups[h]
                n=jnp.where(inblk,0.0,b)
                for k in range(8):
                    n=n-col(b,base+k)*U[k]
                groups[h]=n
    return jnp.concatenate(out,axis=0)

ORTH = (2, 4)


def trace_of(square):
    shape = square.shape
    eye = lax.broadcasted_iota(jnp.int32, shape, 0) == lax.broadcasted_iota(jnp.int32, shape, 1)
    return eye, jnp.sum(jnp.sum(jnp.where(eye, square, 0.0), axis=1, keepdims=True), axis=0, keepdims=True)


def subspace_kernel(z_ref, probe_ref, basis_ref, coeffs_ref, all_ref):
    snaps, weights, group, width = z_ref.shape
    n = snaps * group
    r = probe_ref.shape[1]
    g, p = None, None
    for w in range(weights):
        block = z_ref[:, w].reshape(n, width)
        square = dott(block, block, 1, 1)
        first = dott(block, probe_ref[w * width : (w + 1) * width, :], 1, 0)
        g = square if g is None else g + square
        p = first if p is None else p + first
    mean = trace_of(g)[1] * (1.0 / n)
    g = g * (1.0 / mean)
    for it in range(1, ITERS + 1):
        m = dott(g, p, 1, 0)
        if it in ORTH:
            gram = dott(p, m, 0, 0)
            if it < ITERS:
                eye, total = trace_of(gram)
                gram = gram + jnp.where(eye, total * (2e-6 / r), 0.0)
            inv = inverse_factor(gram)
            last = dott(p, inv, 1, 1)
            p = dott(m, inv, 1, 1)
        else:
            p = m
    scale = lax.rsqrt(mean)
    all_ref[...] = p * (mean * scale)
    mine = coeffs_ref.shape[0]
    place = (lax.axis_index("snap") * weights + lax.axis_index("weight")) * mine
    tile = all_ref[pl.ds(pl.multiple_of(place // 8 * 8, 8), 8), :]
    own = tile[0:mine]
    for q in range(mine, 8, mine):
        own = jnp.where(lax.rem(place, 8) == q, tile[q : q + mine], own)
    coeffs_ref[...] = own
    last = last * scale
    for w in range(weights):
        basis_ref[w * width : (w + 1) * width, :] = dott(z_ref[:, w].reshape(n, width), last, 0, 0)


def subspace(z, probe, mine):
    n = z.shape[0] * z.shape[2]
    r = probe.shape[1]
    return pl.pallas_call(
        subspace_kernel,
        out_shape=(jax.ShapeDtypeStruct(probe.shape, jnp.float32), jax.ShapeDtypeStruct((mine, r), jnp.float32)),
        in_specs=[pl.BlockSpec(memory_space=pltpu.VMEM)] * 2,
        out_specs=[pl.BlockSpec(memory_space=pltpu.VMEM)] * 2,
        scratch_shapes=[pltpu.VMEM((n, r), jnp.float32)],
        compiler_params=pltpu.CompilerParams(vmem_limit_bytes=48 << 20),
    )(z, probe)


CHUNKS = 4


def encode_kernel(
    rows_ref, conv_ref, dense_ref, latents_ref, z_ref,
    land, conv_buf, dense_buf, chosen_ref, voxel, total, partial, landing,
    own_sem, conv_sem, dense_sem, line_send, line_recv, sum_send, sum_recv, row_send, row_recv, far_send, far_recv,
):
    snap, weight = lax.axis_index("snap"), lax.axis_index("weight")
    snaps, weights, group, width = z_ref.shape
    mine = latents_ref.shape[0]
    chunk = land.shape[3]
    voxels = voxel.shape[0]
    mesh_id = pl.DeviceIdType.MESH

    bits = []
    while 2 ** len(bits) < snaps:
        bits.append(2 ** len(bits))

    def flip(bit):
        return snap + bit * (1 - 2 * lax.rem(snap // bit, 2))

    def flips(subset):
        where = snap
        for bit in subset:
            where = where + bit * (1 - 2 * lax.rem(snap // bit, 2))
        return where

    def near(distance):
        return lax.rem(weight + distance, weights)

    own_copies = []
    for c in range(CHUNKS):
        copy = pltpu.make_async_copy(rows_ref.at[:, pl.ds(c * chunk, chunk)], land.at[weight, c], own_sem.at[c])
        copy.start()
        own_copies.append(copy)
    barrier = pltpu.get_barrier_semaphore()
    for d in range(1, weights):
        pl.semaphore_signal(barrier, inc=1, device_id=(snap, near(d)), device_id_type=mesh_id)
    for bit in bits:
        pl.semaphore_signal(barrier, inc=1, device_id=(flip(bit), weight), device_id_type=mesh_id)
    conv_copies = []
    for c in range(CHUNKS):
        copy = pltpu.make_async_copy(
            conv_ref.at[:, pl.ds(1, 2), pl.ds(c * chunk, chunk), :], conv_buf.at[c], conv_sem.at[c]
        )
        copy.start()
        conv_copies.append(copy)
    dense_copy = pltpu.make_async_copy(dense_ref, dense_buf, dense_sem)
    dense_copy.start()
    pl.semaphore_wait(barrier, weights - 1 + len(bits))

    def line_copy(c, d, up):
        source = weight - (d - 1) if up else weight + (d - 1)
        return pltpu.make_async_remote_copy(
            src_ref=land.at[source, c],
            dst_ref=land.at[source, c],
            send_sem=line_send.at[c, d, int(up)],
            recv_sem=line_recv.at[c, d, int(up)],
            device_id=(snap, weight + 1 if up else weight - 1),
            device_id_type=mesh_id,
        )

    def line_sends(d, up):
        if up:
            return (weight + 1 < weights) & (weight - (d - 1) >= 0)
        return (weight - 1 >= 0) & (weight + (d - 1) < weights)

    def send(c, d):
        for up in (True, False):
            @pl.when(line_sends(d, up))
            def _():
                line_copy(c, d, up).start()

    def arrive(c, d):
        for up in (True, False):
            @pl.when(weight - d >= 0 if up else weight + d < weights)
            def _():
                source = weight - d if up else weight + d
                pltpu.make_async_remote_copy(
                    src_ref=land.at[source, c],
                    dst_ref=land.at[source, c],
                    send_sem=line_send.at[c, d, int(up)],
                    recv_sem=line_recv.at[c, d, int(up)],
                    device_id=(snap, weight - 1 if up else weight + 1),
                    device_id_type=mesh_id,
                ).wait_recv()

    for c in range(min(2, CHUNKS)):
        own_copies[c].wait()
        send(c, 1)
    for c in range(2, CHUNKS):
        own_copies[c].wait()

    count = 32 * group
    place = lax.broadcasted_iota(jnp.int32, (count, count), 0)
    source = lax.broadcasted_iota(jnp.int32, (count, count), 1)
    wanted = lax.rem(source, 32) * group + source // 32
    chosen_ref[...] = jnp.where(place == wanted, 1.0, 0.0).astype(jnp.bfloat16)

    def forward(c, d):
        arrive(c, d)
        if d < weights - 1:
            send(c, d + 1)

    for d in range(1, weights):
        forward(0, d)
    for c in range(CHUNKS):
        if c + 2 < CHUNKS:
            send(c + 2, 1)
        rows = land[:, c].reshape(count, chunk)
        moved = jnp.dot(chosen_ref[...], rows, preferred_element_type=jnp.float32)
        voxel[...] = moved.astype(jnp.bfloat16).reshape(voxel.shape)
        conv_copies[c].wait()
        blank = jnp.zeros((group, chunk), jnp.bfloat16)
        for first in range(3):
            columns = []
            for second in range(3):
                for third in range(2):
                    blocks = []
                    for i in range(2):
                        for j in range(2):
                            x, y = 2 * i + first - 1, 2 * j + second - 1
                            blocks.append(blank if x < 0 or y < 0 else voxel[8 * x + 2 * y + third])
                    columns.append(jnp.concatenate(blocks, axis=0))
            patch = jnp.concatenate(columns, axis=1)
            taps = conv_buf[c, 3 * first : 3 * first + 3].reshape(6 * chunk, -1)
            product = jnp.dot(patch, taps, preferred_element_type=jnp.float32)
            if c == 0 and first == 0:
                total[...] = product
            else:
                total[...] += product
            if c + 1 < CHUNKS:
                steps = weights - 1
                for d in range(first * steps // 3 + 1, (first + 1) * steps // 3 + 1):
                    forward(c + 1, d)

    hidden = jnp.tanh(total[...]).astype(jnp.bfloat16)
    hidden = jnp.concatenate([hidden[v * group : (v + 1) * group] for v in range(4)], axis=1)
    dense_copy.wait()

    def partial_sum(distance):
        start = pl.multiple_of(near(distance) * width, width)
        block = dense_buf[:, :, pl.ds(start, width)].reshape(hidden.shape[1], width)
        return jnp.dot(hidden, block, preferred_element_type=jnp.float32)

    sums = []
    for d in range(1, weights):
        partial[d] = partial_sum(d)
        copy = pltpu.make_async_remote_copy(
            src_ref=partial.at[d],
            dst_ref=landing.at[d],
            send_sem=sum_send.at[d],
            recv_sem=sum_recv.at[d],
            device_id=(snap, near(d)),
            device_id_type=mesh_id,
        )
        copy.start()
        sums.append(copy)
    value = partial_sum(0)
    for d in range(1, weights):
        sums[d - 1].wait_recv()
        value = value + landing[d]
    z_ref[snap, weight] = value

    row_copies = []
    for d in range(1, weights):
        copy = pltpu.make_async_remote_copy(
            src_ref=z_ref.at[snap, weight],
            dst_ref=z_ref.at[snap, weight],
            send_sem=row_send.at[d],
            recv_sem=row_recv.at[d],
            device_id=(snap, near(d)),
            device_id_type=mesh_id,
        )
        copy.start()
        row_copies.append(copy)

    far_copies = []

    def route(d):
        off = bits[1:]
        turn = d % len(off) if off else 0
        return off[turn:] + off[:turn] + bits[:1]

    def held(d):
        return lax.rem(weight + weights - d, weights)

    def subsets(stage, order):
        result = [()]
        for bit in order[:stage]:
            result = result + [s + (bit,) for s in result]
        return result

    def far_copy(d, stage, number, subset, to):
        return pltpu.make_async_remote_copy(
            src_ref=z_ref.at[flips(subset), held(d)],
            dst_ref=z_ref.at[flips(subset), held(d)],
            send_sem=far_send.at[d, stage, number],
            recv_sem=far_recv.at[d, stage, number],
            device_id=(to, weight),
            device_id_type=mesh_id,
        )

    def pass_on(d, stage, known):
        order = route(d)
        for number, subset in enumerate(subsets(stage, order)):
            if subset == known:
                copy = far_copy(d, stage, number, subset, flip(order[stage]))
                copy.start()
                far_copies.append(copy)

    for d in range(weights):
        if d:
            row_copies[d - 1].wait_recv()
        for stage in range(len(bits)):
            pass_on(d, stage, ())
    for stage in range(len(bits)):
        for d in range(weights):
            order = route(d)
            for number, subset in enumerate(subsets(stage, order)):
                far_copy(d, stage, number, subset + (order[stage],), flip(order[stage])).wait_recv()
                for later in range(stage + 1, len(bits)):
                    pass_on(d, later, subset + (order[stage],))

    for d in range(weights):
        block = held(d)
        rows = z_ref[snap, block]
        own = rows[0:mine]
        for q in range(1, weights):
            own = jnp.where(weight == q, rows[q * mine : (q + 1) * mine], own)
        latents_ref[:, pl.ds(pl.multiple_of(block * width, width), width)] = own.astype(latents_ref.dtype)

    for copy in sums + row_copies + far_copies:
        copy.wait_send()
    for c in range(CHUNKS):
        for d in range(1, weights):
            for up in (True, False):
                @pl.when(line_sends(d, up))
                def _():
                    line_copy(c, d, up).wait_send()


def encode(rows, conv_weight, dense_weight, snaps, weights, mine):
    channels, local_out = conv_weight.shape[1:]
    latent = dense_weight.shape[-1]
    group = mine * weights
    width = latent // weights
    chunk = channels // CHUNKS
    stages = max(1, (snaps - 1).bit_length())
    hbm = pl.BlockSpec(memory_space=pl.ANY)
    vmem = pl.BlockSpec(memory_space=pltpu.VMEM)
    dma = pltpu.SemaphoreType.DMA
    return pl.pallas_call(
        encode_kernel,
        out_shape=(
            jax.ShapeDtypeStruct((mine, latent), jnp.bfloat16),
            jax.ShapeDtypeStruct((snaps, weights, group, width), jnp.float32),
        ),
        in_specs=[hbm] * 3,
        out_specs=[vmem] * 2,
        scratch_shapes=[
            pltpu.VMEM((weights, CHUNKS, rows.shape[0], chunk), jnp.bfloat16),
            pltpu.VMEM((CHUNKS, 9, 2, chunk, local_out), jnp.bfloat16),
            pltpu.VMEM(dense_weight.shape, jnp.bfloat16),
            pltpu.VMEM((32 * group, 32 * group), jnp.bfloat16),
            pltpu.VMEM((32, group, chunk), jnp.bfloat16),
            pltpu.VMEM((4 * group, local_out), jnp.float32),
            pltpu.VMEM((weights, group, width), jnp.float32),
            pltpu.VMEM((weights, group, width), jnp.float32),
            dma((CHUNKS,)),
            dma((CHUNKS,)),
            dma,
            dma((CHUNKS, weights, 2)),
            dma((CHUNKS, weights, 2)),
            dma((weights,)),
            dma((weights,)),
            dma((weights,)),
            dma((weights,)),
            dma((weights, stages, snaps // 2)),
            dma((weights, stages, snaps // 2)),
        ],
        compiler_params=pltpu.CompilerParams(
            collective_id=0, has_side_effects=True, vmem_limit_bytes=48 << 20
        ),
    )(rows, conv_weight.reshape(9, 3, channels, local_out), dense_weight)


def body(features, conv_weight, dense_weight, probe):
    channels = features.shape[-1]
    mine = features.shape[0]
    snaps, weights = lax.axis_size("snap"), lax.axis_size("weight")
    latents, z = encode(features.reshape(-1, channels), conv_weight, dense_weight, snaps, weights, mine)
    basis, coeffs = subspace(z, probe, mine)
    return latents, basis, coeffs


def solution(mesh):
    placed = (
        P(("snap", "weight"), None, None, None, None),
        P(None, None, "weight"),
        P(None, "weight", None),
        P(),
    )
    return jax.shard_map(
        body,
        mesh=mesh,
        in_specs=placed,
        out_specs=(P(("snap", "weight"), None), P(), P(("snap", "weight"), None)),
        check_vma=False,
    )
```

```python
import functools

import jax
import jax.numpy as jnp
from jax import lax
from jax.experimental import pallas as pl
from jax.experimental.pallas import tpu as pltpu
from jax.sharding import PartitionSpec as P

ITERS = 4
HI = lax.Precision.HIGHEST
def halves(x):
    near = x.astype(jnp.bfloat16)
    return near, (x - near.astype(jnp.float32)).astype(jnp.bfloat16)


def bdot(a, b, ca=1, cb=0):
    return lax.dot_general(a, b, (((ca,), (cb,)), ((), ())), preferred_element_type=jnp.float32)


def dott(a,b,ca,cb):
    return lax.dot_general(a,b,(((ca,),(cb,)),((),())),precision=HI,preferred_element_type=jnp.float32)

def inverse_factor(gram):
    rank = gram.shape[0]
    nb = rank//8
    full=(8,rank)
    groups = [gram[8*g:8*g+8,:] for g in range(nb)]
    lane = lax.broadcasted_iota(jnp.int32,full,1)
    sub = lax.broadcasted_iota(jnp.int32,full,0)
    out=[]
    def col(x,j): return jnp.broadcast_to(x[:,j:j+1],full)
    def row(x,i): return jnp.broadcast_to(x[i:i+1,:],full)
    for g in range(nb):
        panel = groups[g]
        base = 8*g
        inblk = (lane>=base)&(lane<base+8)
        X=[col(panel,base+j) for j in range(8)]
        d=[[row(X[j],i) if j<=i else None for j in range(8)] for i in range(8)]
        panelI = jnp.where(inblk, jnp.where(lane-base==sub,1.0,0.0), panel)
        acc=[row(panelI,i) for i in range(8)]
        nxt = g+1<nb
        if nxt:
            C=[col(groups[g+1],base+k) for k in range(8)]
            new = jnp.where(inblk,0.0,groups[g+1])
        l=[[None]*8 for _ in range(8)]
        r=[None]*8
        W=[None]*8
        for k in range(8):
            r[k]=lax.rsqrt(d[k][k])
            W[k]=acc[k]*r[k]
            if nxt:
                C[k]=C[k]*r[k]
                new = new - C[k]*W[k]
            for i in range(k+1,8):
                l[i][k]=d[i][k]*r[k]
            for i in range(k+1,8):
                for j in range(k+1,i+1):
                    d[i][j]=d[i][j]-l[i][k]*l[j][k]
                acc[i]=acc[i]-l[i][k]*W[k]
                if nxt: C[i]=C[i]-l[i][k]*C[k]
        t=W[0]
        for k in range(1,8):
            t=jnp.where(sub==k,W[k],t)
        out.append(jnp.where(lane<base+8,t,0.0))
        first = g+1
        if nxt:
            groups[g+1]=new
            first=g+2
        if first<nb:
            U=list(W)
            for k in range(7,-1,-1):
                U[k]=U[k]*r[k]
                for i in range(k):
                    U[i]=U[i]-l[k][i]*U[k]
            for h in range(first,nb):
                b=groups[h]
                n=jnp.where(inblk,0.0,b)
                for k in range(8):
                    n=n-col(b,base+k)*U[k]
                groups[h]=n
    return jnp.concatenate(out,axis=0)

ORTH = (2, 4)


def trace_of(square):
    shape = square.shape
    eye = lax.broadcasted_iota(jnp.int32, shape, 0) == lax.broadcasted_iota(jnp.int32, shape, 1)
    return eye, jnp.sum(jnp.sum(jnp.where(eye, square, 0.0), axis=1, keepdims=True), axis=0, keepdims=True)


def subspace_kernel(z_ref, latents_ref, basis_ref, coeffs_ref, all_ref):
    pairs, _, weights, group, _ = z_ref.shape
    n = 2 * pairs * group
    r = coeffs_ref.shape[1]
    width = basis_ref.shape[0] // weights
    g, p = None, None
    for w in range(weights):
        block = z_ref[:, :, w].reshape(n, -1)
        square = bdot(block[:, :width], block[:, :width], 1, 1)
        first = block[:, width : width + r].astype(jnp.float32) + block[:, width + r :].astype(jnp.float32)
        g = square if g is None else g + square
        p = first if p is None else p + first
    mean = trace_of(g)[1] * (1.0 / n)
    g = g * (1.0 / mean)
    for it in range(1, ITERS + 1):
        m = dott(g, p, 1, 0)
        if it in ORTH:
            gram = dott(p, m, 0, 0)
            if it < ITERS:
                eye, total = trace_of(gram)
                gram = gram + jnp.where(eye, total * (2e-6 / r), 0.0)
            inv = inverse_factor(gram)
            last = dott(p, inv, 1, 1)
            p = dott(m, inv, 1, 1)
        else:
            p = m
    scale = lax.rsqrt(mean)
    all_ref[...] = p * (mean * scale)
    mine = coeffs_ref.shape[0]
    snap, weight = lax.axis_index("snap"), lax.axis_index("weight")
    for w in range(weights):
        rows = z_ref[snap // 2, lax.rem(snap, 2), w][:, :width].astype(jnp.float32)
        own = rows[0:mine]
        for q in range(1, weights):
            own = jnp.where(weight == q, rows[q * mine : (q + 1) * mine], own)
        latents_ref[:, w * width : (w + 1) * width] = own.astype(latents_ref.dtype)
    place = (snap * weights + weight) * mine
    tile = all_ref[pl.ds(pl.multiple_of(place // 8 * 8, 8), 8), :]
    own = tile[0:mine]
    for q in range(mine, 8, mine):
        own = jnp.where(lax.rem(place, 8) == q, tile[q : q + mine], own)
    coeffs_ref[...] = own
    last, rest = halves(last * scale)
    for w in range(weights):
        block = z_ref[:, :, w].reshape(n, -1)[:, :width]
        basis_ref[w * width : (w + 1) * width, :] = bdot(block, last, 0, 0) + bdot(block, rest, 0, 0)


def subspace(z, probe, mine):
    n = 2 * z.shape[0] * z.shape[3]
    r = probe.shape[1]
    return pl.pallas_call(
        subspace_kernel,
        out_shape=(
            jax.ShapeDtypeStruct((mine, probe.shape[0]), jnp.bfloat16),
            jax.ShapeDtypeStruct(probe.shape, jnp.float32),
            jax.ShapeDtypeStruct((mine, r), jnp.float32),
        ),
        in_specs=[pl.BlockSpec(memory_space=pltpu.VMEM)],
        out_specs=[pl.BlockSpec(memory_space=pltpu.VMEM)] * 3,
        scratch_shapes=[pltpu.VMEM((n, r), jnp.float32)],
        compiler_params=pltpu.CompilerParams(vmem_limit_bytes=48 << 20),
    )(z)


CHUNKS = 2
SKEW = 1


def encode_kernel(
    rows_ref, conv_ref, dense_ref, probe_ref, z_ref,
    land, conv_buf, dense_buf, probe_buf, chosen_ref, voxel, total, partial, landing,
    own_sem, conv_sem, dense_sem, probe_sem, line_send, line_recv, sum_send, sum_recv, row_send, row_recv, far_send, far_recv,
    twin_send, twin_recv,
):
    snap, weight = lax.axis_index("snap"), lax.axis_index("weight")
    pairs, _, weights, group, _ = z_ref.shape
    width = partial.shape[2]
    snaps = 2 * pairs
    high, low = snap // 2, lax.rem(snap, 2)
    chunk = land.shape[3]
    mesh_id = pl.DeviceIdType.MESH

    bits = []
    while 2 ** len(bits) < snaps:
        bits.append(2 ** len(bits))

    def flip(*subset):
        where = snap
        for bit in subset:
            where = where + bit * (1 - 2 * lax.rem(snap // bit, 2))
        return where

    def near(distance):
        return lax.rem(weight + distance, weights)

    own_copies = []
    for c in range(CHUNKS):
        copy = pltpu.make_async_copy(rows_ref.at[:, pl.ds(c * chunk, chunk)], land.at[weight, c], own_sem.at[c])
        copy.start()
        own_copies.append(copy)
    barrier = pltpu.get_barrier_semaphore()
    for d in range(1, weights):
        pl.semaphore_signal(barrier, inc=1, device_id=(snap, near(d)), device_id_type=mesh_id)
    pl.semaphore_signal(barrier, inc=1, device_id=(flip(1), weight), device_id_type=mesh_id)
    for k in range(1, pairs):
        pl.semaphore_signal(
            barrier, inc=1, device_id=(flip(*[bit for bit in bits if bit & (2 * k)]), weight), device_id_type=mesh_id
        )
    conv_copies = []
    for c in range(CHUNKS):
        copy = pltpu.make_async_copy(
            conv_ref.at[:, pl.ds(1, 2), pl.ds(c * chunk, chunk), :], conv_buf.at[c], conv_sem.at[c]
        )
        copy.start()
        conv_copies.append(copy)
    dense_copy = pltpu.make_async_copy(dense_ref, dense_buf, dense_sem)
    dense_copy.start()
    probe_copy = pltpu.make_async_copy(
        probe_ref.at[pl.ds(pl.multiple_of(weight * width, width), width), :], probe_buf, probe_sem
    )
    probe_copy.start()
    pl.semaphore_wait(barrier, weights + pairs - 1)

    def line_copy(c, d, up):
        source = weight - (d - 1) if up else weight + (d - 1)
        return pltpu.make_async_remote_copy(
            src_ref=land.at[source, c],
            dst_ref=land.at[source, c],
            send_sem=line_send.at[c, d, int(up)],
            recv_sem=line_recv.at[c, d, int(up)],
            device_id=(snap, weight + 1 if up else weight - 1),
            device_id_type=mesh_id,
        )

    def line_sends(d, up):
        if up:
            return (weight + 1 < weights) & (weight - (d - 1) >= 0)
        return (weight - 1 >= 0) & (weight + (d - 1) < weights)

    def send(c, d):
        for up in (True, False):
            @pl.when(line_sends(d, up))
            def _():
                line_copy(c, d, up).start()

    def arrive(c, d):
        for up in (True, False):
            @pl.when(weight - d >= 0 if up else weight + d < weights)
            def _():
                source = weight - d if up else weight + d
                pltpu.make_async_remote_copy(
                    src_ref=land.at[source, c],
                    dst_ref=land.at[source, c],
                    send_sem=line_send.at[c, d, int(up)],
                    recv_sem=line_recv.at[c, d, int(up)],
                    device_id=(snap, weight - 1 if up else weight + 1),
                    device_id_type=mesh_id,
                ).wait_recv()

    for c in range(CHUNKS):
        own_copies[c].wait()
        send(c, 1)

    count = 32 * group
    place = lax.broadcasted_iota(jnp.int32, (count, count), 0)
    source = lax.broadcasted_iota(jnp.int32, (count, count), 1)
    wanted = (source & 31) * group + (source >> 5)
    chosen_ref[...] = jnp.where(place == wanted, 1.0, 0.0).astype(jnp.bfloat16)

    def forward(t, d):
        c = t - SKEW * (d - 1)
        if 0 <= c < CHUNKS:
            arrive(c, d)
            if d < weights - 1:
                send(c, d + 1)

    inner = (weight > 0) & (weight < weights - 1)

    @pl.when(inner)
    def _():
        for t in range(CHUNKS + SKEW * (weights - 2)):
            for d in range(1, weights):
                forward(t, d)

    for c in range(CHUNKS):
        @pl.when(jnp.logical_not(inner))
        def _():
            for d in range(1, weights):
                arrive(c, d)

        rows = land[:, c].reshape(count, chunk)
        moved = jnp.dot(chosen_ref[...], rows, preferred_element_type=jnp.float32)
        voxel[...] = moved.astype(jnp.bfloat16).reshape(voxel.shape)
        conv_copies[c].wait()
        blank = jnp.zeros((group, chunk), jnp.bfloat16)
        for first in range(3):
            columns = []
            for second in range(3):
                for third in range(2):
                    blocks = []
                    for i in range(2):
                        for j in range(2):
                            x, y = 2 * i + first - 1, 2 * j + second - 1
                            blocks.append(blank if x < 0 or y < 0 else voxel[8 * x + 2 * y + third])
                    columns.append(jnp.concatenate(blocks, axis=0))
            patch = jnp.concatenate(columns, axis=1)
            taps = conv_buf[c, 3 * first : 3 * first + 3].reshape(6 * chunk, -1)
            product = jnp.dot(patch, taps, preferred_element_type=jnp.float32)
            if c == 0 and first == 0:
                total[...] = product
            else:
                total[...] += product

    hidden = jnp.tanh(total[...]).astype(jnp.bfloat16)
    hidden = jnp.concatenate([hidden[v * group : (v + 1) * group] for v in range(4)], axis=1)
    dense_copy.wait()

    def partial_sum(distance):
        start = pl.multiple_of(near(distance) * width, width)
        block = dense_buf[:, :, pl.ds(start, width)].reshape(hidden.shape[1], width)
        return jnp.dot(hidden, block, preferred_element_type=jnp.float32)

    sums = []
    for d in range(1, weights):
        partial[d] = partial_sum(d)
        copy = pltpu.make_async_remote_copy(
            src_ref=partial.at[d],
            dst_ref=landing.at[d],
            send_sem=sum_send.at[d],
            recv_sem=sum_recv.at[d],
            device_id=(snap, near(d)),
            device_id_type=mesh_id,
        )
        copy.start()
        sums.append(copy)
    value = partial_sum(0)
    probe_copy.wait()
    for d in range(1, weights):
        sums[d - 1].wait_recv()
        value = value + landing[d]
    near_value, value = halves(value)
    near_probe, rest = halves(probe_buf[...])
    start = bdot(near_value, near_probe) + (bdot(near_value, rest) + bdot(value, near_probe))
    z_ref[high, low, weight] = jnp.concatenate([near_value, *halves(start)], axis=1)

    row_copies = []
    for d in range(1, weights):
        copy = pltpu.make_async_remote_copy(
            src_ref=z_ref.at[high, low, weight],
            dst_ref=z_ref.at[high, low, weight],
            send_sem=row_send.at[d],
            recv_sem=row_recv.at[d],
            device_id=(snap, near(d)),
            device_id_type=mesh_id,
        )
        copy.start()
        row_copies.append(copy)

    far_copies = []

    def held(d):
        return lax.rem(weight + weights - d, weights)

    def hop(k):
        return [bit for bit in bits if bit & (2 * k)]

    def far_copy(d, k):
        block = z_ref.at[high, low, held(d)]
        return pltpu.make_async_remote_copy(
            src_ref=block,
            dst_ref=block,
            send_sem=far_send.at[d, k],
            recv_sem=far_recv.at[d, k],
            device_id=(flip(*hop(k)), weight),
            device_id_type=mesh_id,
        )

    def twin_copy(d, k, side):
        block = z_ref.at[flip(*hop(k)) // 2, side, held(d)]
        return pltpu.make_async_remote_copy(
            src_ref=block,
            dst_ref=block,
            send_sem=twin_send.at[d, k],
            recv_sem=twin_recv.at[d, k],
            device_id=(flip(1), weight),
            device_id_type=mesh_id,
        )

    for d in range(weights):
        if d:
            row_copies[d - 1].wait_recv()
        for k in range(1, pairs):
            far_copies.append(far_copy(d, k))
            far_copies[-1].start()
        far_copies.append(twin_copy(d, 0, low))
        far_copies[-1].start()
    for k in range(1, pairs):
        for d in range(weights):
            block = z_ref.at[flip(*hop(k)) // 2, low, held(d)]
            pltpu.make_async_remote_copy(
                src_ref=block,
                dst_ref=block,
                send_sem=far_send.at[d, k],
                recv_sem=far_recv.at[d, k],
                device_id=(flip(*hop(k)), weight),
                device_id_type=mesh_id,
            ).wait_recv()
            far_copies.append(twin_copy(d, k, low))
            far_copies[-1].start()
    for d in range(weights):
        for k in range(pairs):
            twin_copy(d, k, 1 - low).wait_recv()

    for copy in sums + row_copies + far_copies:
        copy.wait_send()
    for c in range(CHUNKS):
        for d in range(1, weights):
            for up in (True, False):
                @pl.when(line_sends(d, up))
                def _():
                    line_copy(c, d, up).wait_send()


def encode(rows, conv_weight, dense_weight, probe, snaps, weights, mine):
    channels, local_out = conv_weight.shape[1:]
    latent = dense_weight.shape[-1]
    group = mine * weights
    width = latent // weights
    chunk = channels // CHUNKS
    hbm = pl.BlockSpec(memory_space=pltpu.HBM)
    vmem = pl.BlockSpec(memory_space=pltpu.VMEM)
    dma = pltpu.SemaphoreType.DMA
    return pl.pallas_call(
        encode_kernel,
        out_shape=jax.ShapeDtypeStruct((snaps // 2, 2, weights, group, width + 2 * probe.shape[1]), jnp.bfloat16),
        in_specs=[hbm] * 4,
        out_specs=vmem,
        scratch_shapes=[
            pltpu.VMEM((weights, CHUNKS, rows.shape[0], chunk), jnp.bfloat16),
            pltpu.VMEM((CHUNKS, 9, 2, chunk, local_out), jnp.bfloat16),
            pltpu.VMEM(dense_weight.shape, jnp.bfloat16),
            pltpu.VMEM((width, probe.shape[1]), jnp.float32),
            pltpu.VMEM((32 * group, 32 * group), jnp.bfloat16),
            pltpu.VMEM((32, group, chunk), jnp.bfloat16),
            pltpu.VMEM((4 * group, local_out), jnp.float32),
            pltpu.VMEM((weights, group, width), jnp.float32),
            pltpu.VMEM((weights, group, width), jnp.float32),
            dma((CHUNKS,)),
            dma((CHUNKS,)),
            dma,
            dma,
            dma((CHUNKS, weights, 2)),
            dma((CHUNKS, weights, 2)),
            dma((weights,)),
            dma((weights,)),
            dma((weights,)),
            dma((weights,)),
            dma((weights, snaps // 2)),
            dma((weights, snaps // 2)),
            dma((weights, snaps // 2)),
            dma((weights, snaps // 2)),
        ],
        compiler_params=pltpu.CompilerParams(
            collective_id=0, has_side_effects=True, vmem_limit_bytes=48 << 20
        ),
    )(rows, conv_weight.reshape(9, 3, channels, local_out), dense_weight, probe)


def body(features, conv_weight, dense_weight, probe):
    channels = features.shape[-1]
    mine = features.shape[0]
    snaps, weights = lax.axis_size("snap"), lax.axis_size("weight")
    z = encode(features.reshape(-1, channels), conv_weight, dense_weight, probe, snaps, weights, mine)
    return subspace(z, probe, mine)


def solution(mesh):
    placed = (
        P(("snap", "weight"), None, None, None, None),
        P(None, None, "weight"),
        P(None, "weight", None),
        P(),
    )
    return jax.shard_map(
        body,
        mesh=mesh,
        in_specs=placed,
        out_specs=(P(("snap", "weight"), None), P(), P(("snap", "weight"), None)),
        check_vma=False,
    )
```

```python
import functools

import jax
import jax.numpy as jnp
from jax import lax
from jax.experimental import pallas as pl
from jax.experimental.pallas import tpu as pltpu
from jax.sharding import PartitionSpec as P

ITERS = 4
HI = lax.Precision.HIGHEST
def halves(x):
    near = x.astype(jnp.bfloat16)
    return near, (x - near.astype(jnp.float32)).astype(jnp.bfloat16)


def bdot(a, b, ca=1, cb=0):
    return lax.dot_general(a, b, (((ca,), (cb,)), ((), ())), preferred_element_type=jnp.float32)


def dot3(a, b, ca=1, cb=0):
    (x, y), (u, v) = halves(a), halves(b)
    return bdot(x, u, ca, cb) + (bdot(x, v, ca, cb) + bdot(y, u, ca, cb))


def dott(a,b,ca,cb):
    return lax.dot_general(a,b,(((ca,),(cb,)),((),())),precision=HI,preferred_element_type=jnp.float32)

def inverse_factor(gram):
    rank = gram.shape[0]
    nb = rank//8
    full=(8,rank)
    groups = [gram[8*g:8*g+8,:] for g in range(nb)]
    lane = lax.broadcasted_iota(jnp.int32,full,1)
    sub = lax.broadcasted_iota(jnp.int32,full,0)
    out=[]
    def col(x,j): return jnp.broadcast_to(x[:,j:j+1],full)
    def row(x,i): return jnp.broadcast_to(x[i:i+1,:],full)
    for g in range(nb):
        panel = groups[g]
        base = 8*g
        inblk = (lane>=base)&(lane<base+8)
        X=[col(panel,base+j) for j in range(8)]
        d=[[row(X[j],i) if j<=i else None for j in range(8)] for i in range(8)]
        panelI = jnp.where(inblk, jnp.where(lane-base==sub,1.0,0.0), panel)
        acc=[row(panelI,i) for i in range(8)]
        nxt = g+1<nb
        if nxt:
            C=[col(groups[g+1],base+k) for k in range(8)]
            new = jnp.where(inblk,0.0,groups[g+1])
        l=[[None]*8 for _ in range(8)]
        r=[None]*8
        W=[None]*8
        for k in range(0,8,2):
            a,b,c=d[k][k],d[k+1][k],d[k+1][k+1]
            r[k]=lax.rsqrt(a)
            r[k+1]=lax.rsqrt(a*c-b*b)*(a*r[k])
            l[k+1][k]=b*r[k]
            W[k]=acc[k]*r[k]
            W[k+1]=(acc[k+1]-l[k+1][k]*W[k])*r[k+1]
            if nxt:
                C[k]=C[k]*r[k]
                C[k+1]=(C[k+1]-l[k+1][k]*C[k])*r[k+1]
                new=new-C[k]*W[k]-C[k+1]*W[k+1]
            for i in range(k+2,8):
                l[i][k]=d[i][k]*r[k]
                l[i][k+1]=(d[i][k+1]-l[i][k]*l[k+1][k])*r[k+1]
            for i in range(k+2,8):
                for j in range(k+2,i+1):
                    d[i][j]=d[i][j]-l[i][k]*l[j][k]-l[i][k+1]*l[j][k+1]
                acc[i]=acc[i]-l[i][k]*W[k]-l[i][k+1]*W[k+1]
                if nxt: C[i]=C[i]-l[i][k]*C[k]-l[i][k+1]*C[k+1]
        t=W[0]
        for k in range(1,8):
            t=jnp.where(sub==k,W[k],t)
        out.append(jnp.where(lane<base+8,t,0.0))
        first = g+1
        if nxt:
            groups[g+1]=new
            first=g+2
        if first<nb:
            U=list(W)
            for k in range(7,-1,-1):
                U[k]=U[k]*r[k]
                for i in range(k):
                    U[i]=U[i]-l[k][i]*U[k]
            for h in range(first,nb):
                b=groups[h]
                n=jnp.where(inblk,0.0,b)
                for k in range(8):
                    n=n-col(b,base+k)*U[k]
                groups[h]=n
    return jnp.concatenate(out,axis=0)

ORTH = (2, 4)


def trace_of(square):
    shape = square.shape
    eye = lax.broadcasted_iota(jnp.int32, shape, 0) == lax.broadcasted_iota(jnp.int32, shape, 1)
    return eye, jnp.sum(jnp.sum(jnp.where(eye, square, 0.0), axis=1, keepdims=True), axis=0, keepdims=True)


def subspace_kernel(z_ref, latents_ref, basis_ref, coeffs_ref, all_ref):
    pairs, _, weights, group, _ = z_ref.shape
    n = 2 * pairs * group
    r = coeffs_ref.shape[1]
    width = basis_ref.shape[0] // weights
    g, p = None, None
    for w in range(weights):
        block = z_ref[:, :, w].reshape(n, -1)
        square = bdot(block[:, :width], block[:, :width], 1, 1)
        first = block[:, width : width + r].astype(jnp.float32) + block[:, width + r :].astype(jnp.float32)
        g = square if g is None else g + square
        p = first if p is None else p + first
    mean = trace_of(g)[1] * (1.0 / n)
    g = g * (1.0 / mean)
    for it in range(1, ITERS + 1):
        m = dot3(g, p, 1, 0)
        if it in ORTH:
            gram = dott(p, m, 0, 0)
            if it < ITERS:
                eye, total = trace_of(gram)
                level = total * (1.0 / r)
                gram = gram * (1.0 / level) + jnp.where(eye, 2e-6, 0.0)
                p = dot3(m * lax.rsqrt(level), inverse_factor(gram), 1, 1)
            else:
                inv = inverse_factor(gram)
                last = dot3(p, inv, 1, 1)
                p = dot3(m, inv, 1, 1)
        else:
            p = m
    scale = lax.rsqrt(mean)
    all_ref[...] = p * (mean * scale)
    mine = coeffs_ref.shape[0]
    snap, weight = lax.axis_index("snap"), lax.axis_index("weight")
    for w in range(weights):
        rows = z_ref[snap // 2, lax.rem(snap, 2), w][:, :width].astype(jnp.float32)
        own = rows[0:mine]
        for q in range(1, weights):
            own = jnp.where(weight == q, rows[q * mine : (q + 1) * mine], own)
        latents_ref[:, w * width : (w + 1) * width] = own.astype(latents_ref.dtype)
    place = (snap * weights + weight) * mine
    tile = all_ref[pl.ds(pl.multiple_of(place // 8 * 8, 8), 8), :]
    own = tile[0:mine]
    for q in range(mine, 8, mine):
        own = jnp.where(lax.rem(place, 8) == q, tile[q : q + mine], own)
    coeffs_ref[...] = own
    last, rest = halves(last * scale)
    for w in range(weights):
        block = z_ref[:, :, w].reshape(n, -1)[:, :width]
        basis_ref[w * width : (w + 1) * width, :] = bdot(block, last, 0, 0) + bdot(block, rest, 0, 0)


def subspace(z, probe, mine):
    n = 2 * z.shape[0] * z.shape[3]
    r = probe.shape[1]
    return pl.pallas_call(
        subspace_kernel,
        out_shape=(
            jax.ShapeDtypeStruct((mine, probe.shape[0]), jnp.bfloat16),
            jax.ShapeDtypeStruct(probe.shape, jnp.float32),
            jax.ShapeDtypeStruct((mine, r), jnp.float32),
        ),
        in_specs=[pl.BlockSpec(memory_space=pltpu.VMEM)],
        out_specs=[pl.BlockSpec(memory_space=pltpu.VMEM)] * 3,
        scratch_shapes=[pltpu.VMEM((n, r), jnp.float32)],
        compiler_params=pltpu.CompilerParams(vmem_limit_bytes=48 << 20),
    )(z)


SHARES = (2, 1, 1)
SKEW = 1


def encode_kernel(rows_ref, conv_ref, dense_ref, probe_ref, z_ref, *scratch):
    parts = len(SHARES)
    land, conv_buf, voxels = scratch[:parts], scratch[parts : 2 * parts], scratch[2 * parts : 3 * parts]
    (dense_buf, probe_buf, chosen_ref, total, partial, landing,
     own_sem, conv_sem, dense_sem, probe_sem, line_send, line_recv, sum_send, sum_recv, row_send, row_recv,
     far_send, far_recv, twin_send, twin_recv) = scratch[3 * parts :]
    snap, weight = lax.axis_index("snap"), lax.axis_index("weight")
    pairs, _, weights, group, _ = z_ref.shape
    width = partial.shape[2]
    snaps = 2 * pairs
    high, low = snap // 2, lax.rem(snap, 2)
    chunks = [ref.shape[2] for ref in land]
    starts = [sum(chunks[:c]) for c in range(parts)]
    mesh_id = pl.DeviceIdType.MESH

    bits = []
    while 2 ** len(bits) < snaps:
        bits.append(2 ** len(bits))

    def flip(*subset):
        where = snap
        for bit in subset:
            where = where + bit * (1 - 2 * lax.rem(snap // bit, 2))
        return where

    def near(distance):
        return lax.rem(weight + distance, weights)

    own_copies = []
    for c in range(parts):
        copy = pltpu.make_async_copy(rows_ref.at[:, pl.ds(starts[c], chunks[c])], land[c].at[weight], own_sem.at[c])
        copy.start()
        own_copies.append(copy)
    barrier = pltpu.get_barrier_semaphore()
    for d in range(1, weights):
        pl.semaphore_signal(barrier, inc=1, device_id=(snap, near(d)), device_id_type=mesh_id)
    pl.semaphore_signal(barrier, inc=1, device_id=(flip(1), weight), device_id_type=mesh_id)
    for k in range(1, pairs):
        pl.semaphore_signal(
            barrier, inc=1, device_id=(flip(*[bit for bit in bits if bit & (2 * k)]), weight), device_id_type=mesh_id
        )
    conv_copies = []
    for c in range(parts):
        copy = pltpu.make_async_copy(
            conv_ref.at[:, pl.ds(1, 2), pl.ds(starts[c], chunks[c]), :], conv_buf[c], conv_sem.at[c]
        )
        copy.start()
        conv_copies.append(copy)
    dense_copy = pltpu.make_async_copy(dense_ref, dense_buf, dense_sem)
    dense_copy.start()
    probe_copy = pltpu.make_async_copy(
        probe_ref.at[pl.ds(pl.multiple_of(weight * width, width), width), :], probe_buf, probe_sem
    )
    probe_copy.start()
    pl.semaphore_wait(barrier, weights + pairs - 1)

    def line_copy(c, d, up):
        source = weight - (d - 1) if up else weight + (d - 1)
        return pltpu.make_async_remote_copy(
            src_ref=land[c].at[source],
            dst_ref=land[c].at[source],
            send_sem=line_send.at[c, d, int(up)],
            recv_sem=line_recv.at[c, d, int(up)],
            device_id=(snap, weight + 1 if up else weight - 1),
            device_id_type=mesh_id,
        )

    def line_sends(d, up):
        if up:
            return (weight + 1 < weights) & (weight - (d - 1) >= 0)
        return (weight - 1 >= 0) & (weight + (d - 1) < weights)

    def send(c, d):
        for up in (True, False):
            @pl.when(line_sends(d, up))
            def _():
                line_copy(c, d, up).start()

    def arrive(c, d):
        for up in (True, False):
            @pl.when(weight - d >= 0 if up else weight + d < weights)
            def _():
                source = weight - d if up else weight + d
                pltpu.make_async_remote_copy(
                    src_ref=land[c].at[source],
                    dst_ref=land[c].at[source],
                    send_sem=line_send.at[c, d, int(up)],
                    recv_sem=line_recv.at[c, d, int(up)],
                    device_id=(snap, weight - 1 if up else weight + 1),
                    device_id_type=mesh_id,
                ).wait_recv()

    for c in range(parts):
        own_copies[c].wait()
        send(c, 1)

    count = 32 * group
    place = lax.broadcasted_iota(jnp.int32, (count, count), 0)
    source = lax.broadcasted_iota(jnp.int32, (count, count), 1)
    wanted = (source & 31) * group + (source >> 5)
    chosen_ref[...] = jnp.where(place == wanted, 1.0, 0.0).astype(jnp.bfloat16)

    def forward(t, d):
        c = t - SKEW * (d - 1)
        if 0 <= c < parts:
            arrive(c, d)
            if d < weights - 1:
                send(c, d + 1)

    inner = (weight > 0) & (weight < weights - 1)

    @pl.when(inner)
    def _():
        for t in range(parts + SKEW * (weights - 2)):
            for d in range(1, weights):
                forward(t, d)

    for c in range(parts):
        @pl.when(jnp.logical_not(inner))
        def _():
            for d in range(1, weights):
                arrive(c, d)

        chunk, voxel = chunks[c], voxels[c]
        rows = land[c][...].reshape(count, chunk)
        moved = jnp.dot(chosen_ref[...], rows, preferred_element_type=jnp.float32)
        voxel[...] = moved.astype(jnp.bfloat16).reshape(voxel.shape)
        conv_copies[c].wait()
        blank = jnp.zeros((group, chunk), jnp.bfloat16)
        for first in range(3):
            columns = []
            for second in range(3):
                for third in range(2):
                    blocks = []
                    for i in range(2):
                        for j in range(2):
                            x, y = 2 * i + first - 1, 2 * j + second - 1
                            blocks.append(blank if x < 0 or y < 0 else voxel[8 * x + 2 * y + third])
                    columns.append(jnp.concatenate(blocks, axis=0))
            patch = jnp.concatenate(columns, axis=1)
            taps = conv_buf[c][3 * first : 3 * first + 3].reshape(6 * chunk, -1)
            product = jnp.dot(patch, taps, preferred_element_type=jnp.float32)
            if c == 0 and first == 0:
                total[...] = product
            else:
                total[...] += product

    hidden = jnp.tanh(total[...]).astype(jnp.bfloat16)
    hidden = jnp.concatenate([hidden[v * group : (v + 1) * group] for v in range(4)], axis=1)
    dense_copy.wait()

    def partial_sum(distance):
        start = pl.multiple_of(near(distance) * width, width)
        block = dense_buf[:, :, pl.ds(start, width)].reshape(hidden.shape[1], width)
        return jnp.dot(hidden, block, preferred_element_type=jnp.float32)

    sums = []
    for d in range(1, weights):
        partial[d] = partial_sum(d)
        copy = pltpu.make_async_remote_copy(
            src_ref=partial.at[d],
            dst_ref=landing.at[d],
            send_sem=sum_send.at[d],
            recv_sem=sum_recv.at[d],
            device_id=(snap, near(d)),
            device_id_type=mesh_id,
        )
        copy.start()
        sums.append(copy)
    value = partial_sum(0)
    probe_copy.wait()
    for d in range(1, weights):
        sums[d - 1].wait_recv()
        value = value + landing[d]
    near_value, value = halves(value)
    near_probe, rest = halves(probe_buf[...])
    start = bdot(near_value, near_probe) + (bdot(near_value, rest) + bdot(value, near_probe))
    z_ref[high, low, weight] = jnp.concatenate([near_value, *halves(start)], axis=1)

    row_copies = []
    for d in range(1, weights):
        copy = pltpu.make_async_remote_copy(
            src_ref=z_ref.at[high, low, weight],
            dst_ref=z_ref.at[high, low, weight],
            send_sem=row_send.at[d],
            recv_sem=row_recv.at[d],
            device_id=(snap, near(d)),
            device_id_type=mesh_id,
        )
        copy.start()
        row_copies.append(copy)

    far_copies = []

    def held(d):
        return lax.rem(weight + weights - d, weights)

    def hop(k):
        return [bit for bit in bits if bit & (2 * k)]

    def far_copy(d, k):
        block = z_ref.at[high, low, held(d)]
        return pltpu.make_async_remote_copy(
            src_ref=block,
            dst_ref=block,
            send_sem=far_send.at[d, k],
            recv_sem=far_recv.at[d, k],
            device_id=(flip(*hop(k)), weight),
            device_id_type=mesh_id,
        )

    def twin_copy(d, k, side):
        block = z_ref.at[flip(*hop(k)) // 2, side, held(d)]
        return pltpu.make_async_remote_copy(
            src_ref=block,
            dst_ref=block,
            send_sem=twin_send.at[d, k],
            recv_sem=twin_recv.at[d, k],
            device_id=(flip(1), weight),
            device_id_type=mesh_id,
        )

    for d in range(weights):
        if d:
            row_copies[d - 1].wait_recv()
        for k in range(1, pairs):
            far_copies.append(far_copy(d, k))
            far_copies[-1].start()
        far_copies.append(twin_copy(d, 0, low))
        far_copies[-1].start()
    for k in range(1, pairs):
        for d in range(weights):
            block = z_ref.at[flip(*hop(k)) // 2, low, held(d)]
            pltpu.make_async_remote_copy(
                src_ref=block,
                dst_ref=block,
                send_sem=far_send.at[d, k],
                recv_sem=far_recv.at[d, k],
                device_id=(flip(*hop(k)), weight),
                device_id_type=mesh_id,
            ).wait_recv()
            far_copies.append(twin_copy(d, k, low))
            far_copies[-1].start()
    for d in range(weights):
        for k in range(pairs):
            twin_copy(d, k, 1 - low).wait_recv()

    for copy in sums + row_copies + far_copies:
        copy.wait_send()
    for c in range(parts):
        for d in range(1, weights):
            for up in (True, False):
                @pl.when(line_sends(d, up))
                def _():
                    line_copy(c, d, up).wait_send()


def encode(rows, conv_weight, dense_weight, probe, snaps, weights, mine):
    channels, local_out = conv_weight.shape[1:]
    latent = dense_weight.shape[-1]
    group = mine * weights
    width = latent // weights
    chunks = [channels * share // sum(SHARES) for share in SHARES]
    hbm = pl.BlockSpec(memory_space=pltpu.HBM)
    vmem = pl.BlockSpec(memory_space=pltpu.VMEM)
    dma = pltpu.SemaphoreType.DMA
    return pl.pallas_call(
        encode_kernel,
        out_shape=jax.ShapeDtypeStruct((snaps // 2, 2, weights, group, width + 2 * probe.shape[1]), jnp.bfloat16),
        in_specs=[hbm] * 4,
        out_specs=vmem,
        scratch_shapes=[
            *[pltpu.VMEM((weights, rows.shape[0], chunk), jnp.bfloat16) for chunk in chunks],
            *[pltpu.VMEM((9, 2, chunk, local_out), jnp.bfloat16) for chunk in chunks],
            *[pltpu.VMEM((32, group, chunk), jnp.bfloat16) for chunk in chunks],
            pltpu.VMEM(dense_weight.shape, jnp.bfloat16),
            pltpu.VMEM((width, probe.shape[1]), jnp.float32),
            pltpu.VMEM((32 * group, 32 * group), jnp.bfloat16),
            pltpu.VMEM((4 * group, local_out), jnp.float32),
            pltpu.VMEM((weights, group, width), jnp.float32),
            pltpu.VMEM((weights, group, width), jnp.float32),
            dma((len(SHARES),)),
            dma((len(SHARES),)),
            dma,
            dma,
            dma((len(SHARES), weights, 2)),
            dma((len(SHARES), weights, 2)),
            dma((weights,)),
            dma((weights,)),
            dma((weights,)),
            dma((weights,)),
            dma((weights, snaps // 2)),
            dma((weights, snaps // 2)),
            dma((weights, snaps // 2)),
            dma((weights, snaps // 2)),
        ],
        compiler_params=pltpu.CompilerParams(
            collective_id=0, has_side_effects=True, vmem_limit_bytes=52 << 20
        ),
    )(rows, conv_weight.reshape(9, 3, channels, local_out), dense_weight, probe)


def body(features, conv_weight, dense_weight, probe):
    channels = features.shape[-1]
    mine = features.shape[0]
    snaps, weights = lax.axis_size("snap"), lax.axis_size("weight")
    z = encode(features.reshape(-1, channels), conv_weight, dense_weight, probe, snaps, weights, mine)
    return subspace(z, probe, mine)


def solution(mesh):
    placed = (
        P(("snap", "weight"), None, None, None, None),
        P(None, None, "weight"),
        P(None, "weight", None),
        P(),
    )
    return jax.shard_map(
        body,
        mesh=mesh,
        in_specs=placed,
        out_specs=(P(("snap", "weight"), None), P(), P(("snap", "weight"), None)),
        check_vma=False,
    )
```

```python
import functools

import jax
import jax.numpy as jnp
from jax import lax
from jax.experimental import pallas as pl
from jax.experimental.pallas import tpu as pltpu
from jax.sharding import PartitionSpec as P

ITERS = 4
HI = lax.Precision.HIGHEST
def halves(x):
    near = x.astype(jnp.bfloat16)
    return near, (x - near.astype(jnp.float32)).astype(jnp.bfloat16)


def bdot(a, b, ca=1, cb=0):
    return lax.dot_general(a, b, (((ca,), (cb,)), ((), ())), preferred_element_type=jnp.float32)


def dot3(a, b, ca=1, cb=0):
    (x, y), (u, v) = halves(a), halves(b)
    return bdot(x, u, ca, cb) + (bdot(x, v, ca, cb) + bdot(y, u, ca, cb))


def dott(a,b,ca,cb):
    return lax.dot_general(a,b,(((ca,),(cb,)),((),())),precision=HI,preferred_element_type=jnp.float32)

def inverse_factor(gram, held_ref):
    rank = gram.shape[0]
    nb = rank//8
    full=(8,rank)
    groups = [gram[8*g:8*g+8,:] for g in range(nb)]
    lane = lax.broadcasted_iota(jnp.int32,full,1)
    sub = lax.broadcasted_iota(jnp.int32,full,0)
    out=[]
    def col(x,j): return jnp.broadcast_to(x[:,j:j+1],full)
    def spread(i): return jnp.broadcast_to(held_ref[i:i+1,:],full)
    for g in range(nb):
        panel = groups[g]
        base = 8*g
        inblk = (lane>=base)&(lane<base+8)
        X=[col(panel,base+j) for j in range(8)]
        slot=72*(g%4)
        for j in range(8): held_ref[slot+8*j:slot+8*j+8,:]=X[j]
        d=[[spread(slot+8*j+i) if j<=i else None for j in range(8)] for i in range(8)]
        panelI = jnp.where(inblk, jnp.where(lane-base==sub,1.0,0.0), panel)
        held_ref[slot+64:slot+72,:]=panelI
        acc=[spread(slot+64+i) for i in range(8)]
        nxt = g+1<nb
        if nxt:
            C=[col(groups[g+1],base+k) for k in range(8)]
            new = jnp.where(inblk,0.0,groups[g+1])
        l=[[None]*8 for _ in range(8)]
        r=[None]*8
        W=[None]*8
        for k in range(0,8,2):
            a,b,c=d[k][k],d[k+1][k],d[k+1][k+1]
            r[k]=lax.rsqrt(a)
            r[k+1]=lax.rsqrt(a*c-b*b)*(a*r[k])
            l[k+1][k]=b*r[k]
            W[k]=acc[k]*r[k]
            W[k+1]=(acc[k+1]-l[k+1][k]*W[k])*r[k+1]
            if nxt:
                C[k]=C[k]*r[k]
                C[k+1]=(C[k+1]-l[k+1][k]*C[k])*r[k+1]
                new=new-C[k]*W[k]-C[k+1]*W[k+1]
            for i in range(k+2,8):
                l[i][k]=d[i][k]*r[k]
                l[i][k+1]=(d[i][k+1]-l[i][k]*l[k+1][k])*r[k+1]
            for i in range(k+2,8):
                for j in range(k+2,i+1):
                    d[i][j]=d[i][j]-l[i][k]*l[j][k]-l[i][k+1]*l[j][k+1]
                acc[i]=acc[i]-l[i][k]*W[k]-l[i][k+1]*W[k+1]
                if nxt: C[i]=C[i]-l[i][k]*C[k]-l[i][k+1]*C[k+1]
        t=W[0]
        for k in range(1,8):
            t=jnp.where(sub==k,W[k],t)
        out.append(jnp.where(lane<base+8,t,0.0))
        first = g+1
        if nxt:
            groups[g+1]=new
            first=g+2
        if first<nb:
            U=list(W)
            for k in range(7,-1,-1):
                U[k]=U[k]*r[k]
                for i in range(k):
                    U[i]=U[i]-l[k][i]*U[k]
            for h in range(first,nb):
                b=groups[h]
                n=jnp.where(inblk,0.0,b)
                for k in range(8):
                    n=n-col(b,base+k)*U[k]
                groups[h]=n
    return jnp.concatenate(out,axis=0)

def trace_of(square):
    shape = square.shape
    eye = lax.broadcasted_iota(jnp.int32, shape, 0) == lax.broadcasted_iota(jnp.int32, shape, 1)
    return eye, jnp.sum(jnp.sum(jnp.where(eye, square, 0.0), axis=1, keepdims=True), axis=0, keepdims=True)


def subspace_kernel(z_ref, latents_ref, basis_ref, coeffs_ref, all_ref, held_ref):
    pairs, _, weights, group, _ = z_ref.shape
    n = 2 * pairs * group
    r = coeffs_ref.shape[1]
    width = basis_ref.shape[0] // weights
    g, p = None, None
    for w in range(weights):
        block = z_ref[:, :, w].reshape(n, -1)
        square = bdot(block[:, :width], block[:, :width], 1, 1)
        first = block[:, width : width + r].astype(jnp.float32) + block[:, width + r :].astype(jnp.float32)
        g = square if g is None else g + square
        p = first if p is None else p + first
    mean = trace_of(g)[1] * (1.0 / n)
    once = dot3(g, p, 1, 0) * (1.0 / mean)
    g = g * (1.0 / mean)
    twice = dot3(g, g, 1, 0)
    for it in range(2, ITERS + 1, 2):
        if it > 2:
            once = dot3(g, p, 1, 0)
            m = dot3(twice, p, 1, 0)
        else:
            m = dot3(g, once, 1, 0)
        gram = dott(once, m, 0, 0)
        if it < ITERS:
            eye, sum_diagonal = trace_of(gram)
            level = sum_diagonal * (1.0 / r)
            gram = gram * (1.0 / level) + jnp.where(eye, 2e-6, 0.0)
            p = dot3(m * lax.rsqrt(level), inverse_factor(gram, held_ref), 1, 1)
        else:
            inv = inverse_factor(gram, held_ref)
            last = dot3(once, inv, 1, 1)
            p = dot3(m, inv, 1, 1)
    scale = lax.rsqrt(mean)
    all_ref[...] = p * (mean * scale)
    mine = coeffs_ref.shape[0]
    snap, weight = lax.axis_index("snap"), lax.axis_index("weight")
    for w in range(weights):
        rows = z_ref[snap // 2, lax.rem(snap, 2), w][:, :width].astype(jnp.float32)
        own = rows[0:mine]
        for q in range(1, weights):
            own = jnp.where(weight == q, rows[q * mine : (q + 1) * mine], own)
        latents_ref[:, w * width : (w + 1) * width] = own.astype(latents_ref.dtype)
    place = (snap * weights + weight) * mine
    tile = all_ref[pl.ds(pl.multiple_of(place // 8 * 8, 8), 8), :]
    own = tile[0:mine]
    for q in range(mine, 8, mine):
        own = jnp.where(lax.rem(place, 8) == q, tile[q : q + mine], own)
    coeffs_ref[...] = own
    last, rest = halves(last * scale)
    for w in range(weights):
        block = z_ref[:, :, w].reshape(n, -1)[:, :width]
        basis_ref[w * width : (w + 1) * width, :] = bdot(block, last, 0, 0) + bdot(block, rest, 0, 0)


def subspace(z, probe, mine):
    n = 2 * z.shape[0] * z.shape[3]
    r = probe.shape[1]
    return pl.pallas_call(
        subspace_kernel,
        out_shape=(
            jax.ShapeDtypeStruct((mine, probe.shape[0]), jnp.bfloat16),
            jax.ShapeDtypeStruct(probe.shape, jnp.float32),
            jax.ShapeDtypeStruct((mine, r), jnp.float32),
        ),
        in_specs=[pl.BlockSpec(memory_space=pltpu.VMEM)],
        out_specs=[pl.BlockSpec(memory_space=pltpu.VMEM)] * 3,
        scratch_shapes=[pltpu.VMEM((n, r), jnp.float32), pltpu.VMEM((288, r), jnp.float32)],
        compiler_params=pltpu.CompilerParams(vmem_limit_bytes=48 << 20),
    )(z)


SHARES = (2, 1, 1)
SKEW = 1


def encode_kernel(rows_ref, conv_ref, dense_ref, probe_ref, z_ref, *scratch):
    parts = len(SHARES)
    land, conv_buf, voxels = scratch[:parts], scratch[parts : 2 * parts], scratch[2 * parts : 3 * parts]
    (dense_buf, probe_buf, chosen_ref, total, partial, landing,
     own_sem, conv_sem, dense_sem, probe_sem, line_send, line_recv, sum_send, sum_recv, row_send, row_recv,
     far_send, far_recv, twin_send, twin_recv) = scratch[3 * parts :]
    snap, weight = lax.axis_index("snap"), lax.axis_index("weight")
    pairs, _, weights, group, _ = z_ref.shape
    width = partial.shape[2]
    snaps = 2 * pairs
    high, low = snap // 2, lax.rem(snap, 2)
    chunks = [ref.shape[2] for ref in land]
    starts = [sum(chunks[:c]) for c in range(parts)]
    mesh_id = pl.DeviceIdType.MESH

    bits = []
    while 2 ** len(bits) < snaps:
        bits.append(2 ** len(bits))

    def flip(*subset):
        where = snap
        for bit in subset:
            where = where + bit * (1 - 2 * lax.rem(snap // bit, 2))
        return where

    def near(distance):
        return lax.rem(weight + distance, weights)

    own_copies = []
    for c in range(parts):
        copy = pltpu.make_async_copy(rows_ref.at[:, pl.ds(starts[c], chunks[c])], land[c].at[weight], own_sem.at[c])
        copy.start()
        own_copies.append(copy)
    barrier = pltpu.get_barrier_semaphore()
    for d in range(1, weights):
        pl.semaphore_signal(barrier, inc=1, device_id=(snap, near(d)), device_id_type=mesh_id)
    pl.semaphore_signal(barrier, inc=1, device_id=(flip(1), weight), device_id_type=mesh_id)
    for k in range(1, pairs):
        pl.semaphore_signal(
            barrier, inc=1, device_id=(flip(*[bit for bit in bits if bit & (2 * k)]), weight), device_id_type=mesh_id
        )
    conv_copies = []
    for c in range(parts):
        copy = pltpu.make_async_copy(
            conv_ref.at[:, pl.ds(1, 2), pl.ds(starts[c], chunks[c]), :], conv_buf[c], conv_sem.at[c]
        )
        copy.start()
        conv_copies.append(copy)
    dense_copy = pltpu.make_async_copy(dense_ref, dense_buf, dense_sem)
    dense_copy.start()
    probe_copy = pltpu.make_async_copy(
        probe_ref.at[pl.ds(pl.multiple_of(weight * width, width), width), :], probe_buf, probe_sem
    )
    probe_copy.start()
    pl.semaphore_wait(barrier, weights + pairs - 1)

    def line_copy(c, d, up):
        source = weight - (d - 1) if up else weight + (d - 1)
        return pltpu.make_async_remote_copy(
            src_ref=land[c].at[source],
            dst_ref=land[c].at[source],
            send_sem=line_send.at[c, d, int(up)],
            recv_sem=line_recv.at[c, d, int(up)],
            device_id=(snap, weight + 1 if up else weight - 1),
            device_id_type=mesh_id,
        )

    def line_sends(d, up):
        if up:
            return (weight + 1 < weights) & (weight - (d - 1) >= 0)
        return (weight - 1 >= 0) & (weight + (d - 1) < weights)

    def send(c, d):
        for up in (True, False):
            @pl.when(line_sends(d, up))
            def _():
                line_copy(c, d, up).start()

    def arrive(c, d):
        for up in (True, False):
            @pl.when(weight - d >= 0 if up else weight + d < weights)
            def _():
                source = weight - d if up else weight + d
                pltpu.make_async_remote_copy(
                    src_ref=land[c].at[source],
                    dst_ref=land[c].at[source],
                    send_sem=line_send.at[c, d, int(up)],
                    recv_sem=line_recv.at[c, d, int(up)],
                    device_id=(snap, weight - 1 if up else weight + 1),
                    device_id_type=mesh_id,
                ).wait_recv()

    for c in range(parts):
        own_copies[c].wait()
        send(c, 1)

    count = 32 * group
    place = lax.broadcasted_iota(jnp.int32, (count, count), 0)
    source = lax.broadcasted_iota(jnp.int32, (count, count), 1)
    wanted = (source & 31) * group + (source >> 5)
    chosen_ref[...] = jnp.where(place == wanted, 1.0, 0.0).astype(jnp.bfloat16)

    def forward(t, d):
        c = t - SKEW * (d - 1)
        if 0 <= c < parts:
            arrive(c, d)
            if d < weights - 1:
                send(c, d + 1)

    inner = (weight > 0) & (weight < weights - 1)

    @pl.when(inner)
    def _():
        for t in range(parts + SKEW * (weights - 2)):
            for d in range(1, weights):
                forward(t, d)

    for c in range(parts):
        @pl.when(jnp.logical_not(inner))
        def _():
            for d in range(1, weights):
                arrive(c, d)

        chunk, voxel = chunks[c], voxels[c]
        rows = land[c][...].reshape(count, chunk)
        moved = jnp.dot(chosen_ref[...], rows, preferred_element_type=jnp.float32)
        voxel[...] = moved.astype(jnp.bfloat16).reshape(voxel.shape)
        conv_copies[c].wait()
        blank = jnp.zeros((group, chunk), jnp.bfloat16)
        for first in range(3):
            columns = []
            for second in range(3):
                for third in range(2):
                    blocks = []
                    for i in range(2):
                        for j in range(2):
                            x, y = 2 * i + first - 1, 2 * j + second - 1
                            blocks.append(blank if x < 0 or y < 0 else voxel[8 * x + 2 * y + third])
                    columns.append(jnp.concatenate(blocks, axis=0))
            patch = jnp.concatenate(columns, axis=1)
            taps = conv_buf[c][3 * first : 3 * first + 3].reshape(6 * chunk, -1)
            product = jnp.dot(patch, taps, preferred_element_type=jnp.float32)
            if c == 0 and first == 0:
                total[...] = product
            else:
                total[...] += product

    hidden = jnp.tanh(total[...]).astype(jnp.bfloat16)
    hidden = jnp.concatenate([hidden[v * group : (v + 1) * group] for v in range(4)], axis=1)
    dense_copy.wait()

    def partial_sum(distance):
        start = pl.multiple_of(near(distance) * width, width)
        block = dense_buf[:, :, pl.ds(start, width)].reshape(hidden.shape[1], width)
        return jnp.dot(hidden, block, preferred_element_type=jnp.float32)

    sums = []
    for d in range(1, weights):
        partial[d] = partial_sum(d)
        copy = pltpu.make_async_remote_copy(
            src_ref=partial.at[d],
            dst_ref=landing.at[d],
            send_sem=sum_send.at[d],
            recv_sem=sum_recv.at[d],
            device_id=(snap, near(d)),
            device_id_type=mesh_id,
        )
        copy.start()
        sums.append(copy)
    value = partial_sum(0)
    probe_copy.wait()
    for d in range(1, weights):
        sums[d - 1].wait_recv()
        value = value + landing[d]
    near_value, value = halves(value)
    near_probe, rest = halves(probe_buf[...])
    start = bdot(near_value, near_probe) + (bdot(near_value, rest) + bdot(value, near_probe))
    z_ref[high, low, weight] = jnp.concatenate([near_value, *halves(start)], axis=1)

    row_copies = []
    for d in range(1, weights):
        copy = pltpu.make_async_remote_copy(
            src_ref=z_ref.at[high, low, weight],
            dst_ref=z_ref.at[high, low, weight],
            send_sem=row_send.at[d],
            recv_sem=row_recv.at[d],
            device_id=(snap, near(d)),
            device_id_type=mesh_id,
        )
        copy.start()
        row_copies.append(copy)

    far_copies = []

    def held(d):
        return lax.rem(weight + weights - d, weights)

    def hop(k):
        return [bit for bit in bits if bit & (2 * k)]

    def far_copy(d, k):
        block = z_ref.at[high, low, held(d)]
        return pltpu.make_async_remote_copy(
            src_ref=block,
            dst_ref=block,
            send_sem=far_send.at[d, k],
            recv_sem=far_recv.at[d, k],
            device_id=(flip(*hop(k)), weight),
            device_id_type=mesh_id,
        )

    def twin_copy(d, k, side):
        block = z_ref.at[flip(*hop(k)) // 2, side, held(d)]
        return pltpu.make_async_remote_copy(
            src_ref=block,
            dst_ref=block,
            send_sem=twin_send.at[d, k],
            recv_sem=twin_recv.at[d, k],
            device_id=(flip(1), weight),
            device_id_type=mesh_id,
        )

    for d in range(weights):
        if d:
            row_copies[d - 1].wait_recv()
        for k in range(1, pairs):
            far_copies.append(far_copy(d, k))
            far_copies[-1].start()
        far_copies.append(twin_copy(d, 0, low))
        far_copies[-1].start()
    for k in range(1, pairs):
        for d in range(weights):
            block = z_ref.at[flip(*hop(k)) // 2, low, held(d)]
            pltpu.make_async_remote_copy(
                src_ref=block,
                dst_ref=block,
                send_sem=far_send.at[d, k],
                recv_sem=far_recv.at[d, k],
                device_id=(flip(*hop(k)), weight),
                device_id_type=mesh_id,
            ).wait_recv()
            far_copies.append(twin_copy(d, k, low))
            far_copies[-1].start()
    for d in range(weights):
        for k in range(pairs):
            twin_copy(d, k, 1 - low).wait_recv()

    for copy in sums + row_copies + far_copies:
        copy.wait_send()
    for c in range(parts):
        for d in range(1, weights):
            for up in (True, False):
                @pl.when(line_sends(d, up))
                def _():
                    line_copy(c, d, up).wait_send()


def encode(rows, conv_weight, dense_weight, probe, snaps, weights, mine):
    channels, local_out = conv_weight.shape[1:]
    latent = dense_weight.shape[-1]
    group = mine * weights
    width = latent // weights
    chunks = [channels * share // sum(SHARES) for share in SHARES]
    hbm = pl.BlockSpec(memory_space=pltpu.HBM)
    vmem = pl.BlockSpec(memory_space=pltpu.VMEM)
    dma = pltpu.SemaphoreType.DMA
    return pl.pallas_call(
        encode_kernel,
        out_shape=jax.ShapeDtypeStruct((snaps // 2, 2, weights, group, width + 2 * probe.shape[1]), jnp.bfloat16),
        in_specs=[hbm] * 4,
        out_specs=vmem,
        scratch_shapes=[
            *[pltpu.VMEM((weights, rows.shape[0], chunk), jnp.bfloat16) for chunk in chunks],
            *[pltpu.VMEM((9, 2, chunk, local_out), jnp.bfloat16) for chunk in chunks],
            *[pltpu.VMEM((32, group, chunk), jnp.bfloat16) for chunk in chunks],
            pltpu.VMEM(dense_weight.shape, jnp.bfloat16),
            pltpu.VMEM((width, probe.shape[1]), jnp.float32),
            pltpu.VMEM((32 * group, 32 * group), jnp.bfloat16),
            pltpu.VMEM((4 * group, local_out), jnp.float32),
            pltpu.VMEM((weights, group, width), jnp.float32),
            pltpu.VMEM((weights, group, width), jnp.float32),
            dma((len(SHARES),)),
            dma((len(SHARES),)),
            dma,
            dma,
            dma((len(SHARES), weights, 2)),
            dma((len(SHARES), weights, 2)),
            dma((weights,)),
            dma((weights,)),
            dma((weights,)),
            dma((weights,)),
            dma((weights, snaps // 2)),
            dma((weights, snaps // 2)),
            dma((weights, snaps // 2)),
            dma((weights, snaps // 2)),
        ],
        compiler_params=pltpu.CompilerParams(
            collective_id=0, has_side_effects=True, vmem_limit_bytes=52 << 20
        ),
    )(rows, conv_weight.reshape(9, 3, channels, local_out), dense_weight, probe)


def body(features, conv_weight, dense_weight, probe):
    channels = features.shape[-1]
    mine = features.shape[0]
    snaps, weights = lax.axis_size("snap"), lax.axis_size("weight")
    z = encode(features.reshape(-1, channels), conv_weight, dense_weight, probe, snaps, weights, mine)
    return subspace(z, probe, mine)


def solution(mesh):
    placed = (
        P(("snap", "weight"), None, None, None, None),
        P(None, None, "weight"),
        P(None, "weight", None),
        P(),
    )
    return jax.shard_map(
        body,
        mesh=mesh,
        in_specs=placed,
        out_specs=(P(("snap", "weight"), None), P(), P(("snap", "weight"), None)),
        check_vma=False,
    )
```
